512 devices in a mesh: srow: 32 (over y, x), scol: 16 (over z, core).
Axes of the slice: x: 4, y: 8, z: 8, core: 2. Of those that a mesh axis runs over, the one named last changes fastest.
Arguments:
- leaf_rhs: bfloat16 [32, 16, 4, 256, 512], P('srow', 'scol'), may hold values from -6 to 6
- leaf_inverse: bfloat16 [32, 16, 4, 256, 256], P('srow', 'scol'), may hold values from -0.375 to 0.375
- leaf_blocks: bfloat16 [32, 16, 4, 3, 256, 256], P('srow', 'scol'), may hold values from -0.1875 to 0.1875
- leaf_outer: bfloat16 [32, 16, 4, 256, 256], P('srow', 'scol'), may hold values from -0.046875 to 0.046875
- leaf_targets: int32 [32, 16, 4, 4], P('srow', 'scol'), may hold values 0 or 1
- level_one: bfloat16 [4096, 16, 4, 256], P('srow', 'scol'), may hold values from -0.25 to 0.25
- level_two: bfloat16 [2048, 16, 3, 256], P('srow', 'scol'), may hold values from -0.1875 to 0.1875
- level_three: bfloat16 [1024, 16, 2, 256], P('srow', 'scol'), may hold values from -0.125 to 0.125
Outputs:
- solved_one: bfloat16 [256, 16, 8192], P(None, 'scol', 'srow')
- solved_two: bfloat16 [256, 16, 4096], P(None, 'scol', 'srow')
- solved_three: bfloat16 [256, 16, 2048], P(None, 'scol', 'srow')
- outer_update: float32 [256, 2048], P('scol', 'srow')
The draws below stay inside these ranges and needn't reach their ends.
Inputs may be any that keep to these rules, and one draw needn't show every extreme that they name: `leaf_targets`: 1 marks a block that is present in the leaf's panel, 0 one that is absent.
All inputs are finite; a program needn't handle non-finite values.
Results may differ from the reference program's by a relative error of at most 0.0049.
Values may be sent and summed in bfloat16 or wider, within the bound.
No kernel may reach another device: no remote copies, remote signals or barrier semaphores. Data moves between devices by JAX's collectives and lax.ppermute only.
A program may use at most 64 MiB of HBM per device.

```python
import jax
import jax.numpy as jnp
from jax import lax

BLOCK = 256
COLUMNS = 512
LEAVES = 4
ROW_GROUPS = 32
COL_GROUPS = 16


def place_ends(values, stream_key, low, high):
    extent = values.shape
    index_at = [jax.random.randint(jax.random.fold_in(stream_key, axis), (), 0, extent[axis]) for axis in range(len(extent))]
    values = values.at[tuple(index_at)].set(low)
    longest = extent.index(max(extent))
    index_at[longest] = (index_at[longest] + 1) % extent[longest]
    return values.at[tuple(index_at)].set(high)


def shard_levels(key, extent, shards, low, top_value):
    gain = 1.0
    for axis_at, parts in shards:
        steps = jax.random.uniform(jax.random.fold_in(jax.random.fold_in(key, 6), axis_at), (parts,), jnp.float32, low / len(shards), top_value / len(shards))
        gain = gain * jnp.repeat(jnp.exp(steps), extent[axis_at] // parts).reshape((-1,) + (1,) * (len(extent) - 1 - axis_at))
    return gain


def gaussian(key, shape, spread, most, split=(), dtype=jnp.bfloat16):
    values = jax.random.normal(key, shape, jnp.float32) * spread
    if len(split) > 0:
        values = shard_levels(key, shape, split, -0.22, 0.18) * values
    return jnp.clip(values, min=-most, max=most).astype(dtype)


def setup_inputs(seed: int = 0) -> dict:
    key_of = jax.random.split(jax.random.key(seed), 9)
    return {
        "leaf_rhs": gaussian(key_of[0], (ROW_GROUPS, COL_GROUPS, LEAVES, BLOCK, COLUMNS), 1.0, 6.0, ((0, 32), (1, 16))),
        "leaf_inverse": gaussian(key_of[1], (ROW_GROUPS, COL_GROUPS, LEAVES, BLOCK, BLOCK), BLOCK ** -0.5, 0.375, ((0, 32), (1, 16))),
        "leaf_blocks": gaussian(key_of[2], (ROW_GROUPS, COL_GROUPS, LEAVES, 3, BLOCK, BLOCK), (4 * BLOCK) ** -0.5, 0.1875, ((0, 32), (1, 16))),
        "leaf_outer": gaussian(key_of[3], (ROW_GROUPS, COL_GROUPS, LEAVES, BLOCK, BLOCK), (64 * BLOCK) ** -0.5, 0.046875, ((0, 32), (1, 16))),
        "leaf_targets": place_ends((jax.random.randint(key_of[4], (ROW_GROUPS, COL_GROUPS, LEAVES, 4), 0, 4) < 3).astype(jnp.int32), jax.random.fold_in(key_of[4], 1), 0, 1),
        "level_one": gaussian(key_of[5], (ROW_GROUPS * BLOCK // 2, COL_GROUPS, 4, BLOCK), (2 * BLOCK) ** -0.5, 0.25, ((0, 32), (1, 16))),
        "level_two": gaussian(key_of[6], (ROW_GROUPS * BLOCK // 4, COL_GROUPS, 3, BLOCK), (4 * BLOCK) ** -0.5, 0.1875, ((0, 32), (1, 16))),
        "level_three": gaussian(key_of[7], (ROW_GROUPS * BLOCK // 8, COL_GROUPS, 2, BLOCK), (8 * BLOCK) ** -0.5, 0.125, ((0, 32), (1, 16))),
    }


def to_float(array):
    return array.astype(jnp.float32)


def solve_level(inverse, summed):
    product = jnp.einsum('pcab,pcbn->pcan', to_float(inverse), summed, precision=lax.Precision.HIGHEST)
    return -product


def apply_block(matrix, solution):
    return jnp.einsum('pcab,pcbn->pcan', to_float(matrix), solution, precision=lax.Precision.HIGHEST)


def share_order(array, level_depth):
    width = COLUMNS // 8
    lead = array.shape[:-1]
    shaped = array.reshape(lead + (8 >> level_depth, 1 << level_depth, width))
    return jnp.swapaxes(shaped, -3, -2).reshape(lead + (COLUMNS,))


def solve_group(pieces):
    rhs_part, inverse, blocks, outer_blocks, targets, stack_one, stack_two, stack_three = pieces
    columns = rhs_part.shape[1]
    weights = targets.astype(jnp.float32)
    leaf_solution = jnp.einsum('icjab,icjbn->icjan', to_float(inverse), to_float(rhs_part)).astype(jnp.bfloat16)
    wide_solution = to_float(leaf_solution)
    level_terms = jnp.einsum('icjtab,icjt,icjbn->tican', to_float(blocks), weights[..., :3], wide_solution)
    outer_terms = jnp.einsum('icjab,icj,icjbn->can', to_float(outer_blocks), weights[..., 3], wide_solution)
    matrices_one = jnp.transpose(stack_one, (3, 0, 2, 1, 4))
    matrices_two = jnp.transpose(stack_two, (3, 0, 2, 1, 4))
    matrices_three = jnp.transpose(stack_three, (3, 0, 2, 1, 4))
    sum_one = level_terms[0].reshape(4, 2, columns, BLOCK, COLUMNS).sum(axis=1)
    first_level = solve_level(matrices_one[0], sum_one)
    carried_two = apply_block(matrices_one[1], first_level).reshape(2, 2, columns, BLOCK, COLUMNS).sum(axis=1)
    sum_two = level_terms[1].reshape(2, 4, columns, BLOCK, COLUMNS).sum(axis=1) + carried_two
    second_level = solve_level(matrices_two[0], sum_two)
    sum_three = (level_terms[2].sum(axis=0, keepdims=True)
                 + apply_block(matrices_one[2], first_level).sum(axis=0, keepdims=True)
                 + apply_block(matrices_two[1], second_level).sum(axis=0, keepdims=True))
    third_level = solve_level(matrices_three[0], sum_three)
    outer_sum = (outer_terms
                 + apply_block(matrices_one[3], first_level).sum(axis=0)
                 + apply_block(matrices_two[2], second_level).sum(axis=0)
                 + apply_block(matrices_three[1], third_level)[0])
    return (first_level.astype(jnp.bfloat16), second_level.astype(jnp.bfloat16),
            third_level.astype(jnp.bfloat16), outer_sum.sum(axis=0))


def reference(leaf_rhs, leaf_inverse, leaf_blocks, leaf_outer, leaf_targets, level_one, level_two, level_three):
    groups = ROW_GROUPS // 8
    columns = COL_GROUPS

    def split_rows(array):
        return array.reshape((groups, 8) + array.shape[1:])

    pieces = (split_rows(leaf_rhs), split_rows(leaf_inverse), split_rows(leaf_blocks),
              split_rows(leaf_outer), split_rows(leaf_targets),
              level_one.reshape(groups, 4, BLOCK, columns, 4, BLOCK),
              level_two.reshape(groups, 2, BLOCK, columns, 3, BLOCK),
              level_three.reshape(groups, 1, BLOCK, columns, 2, BLOCK))
    first_all, second_all, third_all, outer_all = lax.map(solve_group, pieces)
    first_all = share_order(first_all, 1)
    second_all = share_order(second_all, 2)
    third_all = share_order(third_all, 3)
    solved_one = jnp.transpose(first_all, (3, 2, 0, 1, 4)).reshape(BLOCK, columns, groups * 4 * COLUMNS)
    solved_two = jnp.transpose(second_all, (3, 2, 0, 1, 4)).reshape(BLOCK, columns, groups * 2 * COLUMNS)
    solved_three = jnp.transpose(third_all, (3, 2, 0, 1, 4)).reshape(BLOCK, columns, groups * COLUMNS)
    outer_update = jnp.transpose(outer_all, (1, 0, 2)).reshape(BLOCK, groups * COLUMNS)
    return solved_one, solved_two, solved_three, outer_update
```

```python
import jax
import jax.numpy as jnp
from jax import lax
from jax.experimental import pallas as pl
from jax.experimental.pallas import tpu as pltpu
from jax.sharding import PartitionSpec as P

F32 = jnp.float32
BF16 = jnp.bfloat16
LEAF_BYTES = 12 << 20
TRANSFORM_BYTES = 6 << 20
SMALL_BYTES = 4 << 20
GROUPS_8 = [[g * 8 + i for i in range(8)] for g in range(4)]
GROUPS_4 = [[g * 4 + i for i in range(4)] for g in range(8)]


def in_vmem(x):
    return pltpu.with_memory_space_constraint(x, pltpu.VMEM)


def in_hbm(x):
    return pltpu.with_memory_space_constraint(x, pltpu.HBM)


def dot(a, b):
    return jnp.dot(a, b, preferred_element_type=F32)


def dot_wide(a, b):
    high = b.astype(BF16)
    low = (b - high.astype(F32)).astype(BF16)
    return dot(a, high) + dot(a, low)


def low_lanes(shape):
    return lax.broadcasted_iota(jnp.int32, shape, 1) < 64


def join_halves(first, second, upper):
    low = low_lanes(first.shape)
    if upper:
        return jnp.where(low, pltpu.roll(first, 64, 1), second)
    return jnp.where(low, first, pltpu.roll(second, 64, 1))


def tile(ref, t):
    return ref[:, t * 128 : (t + 1) * 128]


def leaf_kernel(
    w_ref, inv_hbm, rhs_hbm, blk_hbm, out_hbm,
    t1_ref, t2_ref, t3_ref, o_ref, sent_ref,
    inv, rhs, blk, out, y, masked, sems,
):
    copies = []
    for j in range(4):
        pairs = ((inv_hbm, inv), (rhs_hbm, rhs), (blk_hbm, blk), (out_hbm, out))
        copies.append([pltpu.make_async_copy(a.at[j], b.at[j], sems.at[j, i]) for i, (a, b) in enumerate(pairs)])
    for first in (0, 2):
        for j in range(4):
            for copy in copies[j][first : first + 2]:
                copy.start()
    for j in range(4):
        copies[j][0].wait()
        copies[j][1].wait()
        y[j * 256 : (j + 1) * 256, :] = dot(inv[j], rhs[j]).astype(BF16)
    for j in range(4):
        copies[j][2].wait()
        copies[j][3].wait()
        for t in range(4):
            block = blk[j, t] if t < 3 else out[j]
            masked[t, :, j * 256 : (j + 1) * 256] = block * w_ref[j, t].astype(F32).astype(BF16)
    for t, into in enumerate((t1_ref, t2_ref, t3_ref, o_ref)):
        into[...] = dot(masked[t], y[...]).astype(into.dtype)
    for half in range(2):
        sent_ref[:, half * 128 : (half + 1) * 128] = own_and_other(t1_ref, half)[1].astype(BF16)


def own_and_other(t1_ref, half):
    first, second = tile(t1_ref, 2 * half).astype(F32), tile(t1_ref, 2 * half + 1).astype(F32)
    even = join_halves(first, second, False)
    odd = join_halves(first, second, True)
    own_upper = (lax.axis_index("srow") & 1) == 1
    return jnp.where(own_upper, odd, even), jnp.where(own_upper, even, odd)


def leaf_terms(weights, inverse, rhs, blocks, outer):
    full = pltpu.VMEM((256, 512), F32)
    return pl.pallas_call(
        leaf_kernel,
        name="leaf",
        in_specs=[pl.BlockSpec(memory_space=pltpu.SMEM)] + [pl.BlockSpec(memory_space=pl.ANY)] * 4,
        out_shape=[pltpu.VMEM((256, 512), BF16), full, full, full, pltpu.VMEM((256, 256), BF16)],
        scratch_shapes=[
            pltpu.VMEM((4, 256, 256), BF16),
            pltpu.VMEM((4, 256, 512), BF16),
            pltpu.VMEM((4, 3, 256, 256), BF16),
            pltpu.VMEM((4, 256, 256), BF16),
            pltpu.VMEM((1024, 512), BF16),
            pltpu.VMEM((4, 256, 1024), BF16),
            pltpu.SemaphoreType.DMA((4, 4)),
        ],
        compiler_params=pltpu.CompilerParams(vmem_limit_bytes=LEAF_BYTES),
        cost_estimate=pl.CostEstimate(flops=1_342_177_280, bytes_accessed=6_000_000, transcendentals=0),
    )(in_hbm(weights), in_hbm(inverse), in_hbm(rhs), in_hbm(blocks), in_hbm(outer))


def first_kernel(t1_ref, t2_ref, t3_ref, o_ref, m1_ref, m1r_ref, t2n_ref, t3n_ref, on_ref, d1_ref, one):
    row = lax.axis_index("srow")
    own = pl.multiple_of((row & 1) * 128, 128)
    other = pl.multiple_of(128 - (row & 1) * 128, 128)
    for slot in range(4):
        into = d1_ref if slot == 0 else one.at[slot - 1]
        into[pl.ds(own, 128), :] = m1_ref[:, slot, :]
        into[pl.ds(other, 128), :] = m1r_ref[:, slot, :]
    x1 = dot(d1_ref[...], t1_ref[...]).astype(BF16)
    under = dot(one[...].reshape(768, 256), x1)
    t2n_ref[...] = t2_ref[...] - under[:256]
    t3n_ref[...] = t3_ref[...] - under[256:512]
    on_ref[...] = o_ref[...] - under[512:]


def first_level(t1, t2, t3, o, m1, m1r):
    full = pltpu.VMEM((256, 512), F32)
    return pl.pallas_call(
        first_kernel,
        name="first",
        out_shape=[full, full, full, pltpu.VMEM((256, 256), BF16)],
        scratch_shapes=[pltpu.VMEM((3, 256, 256), BF16)],
        input_output_aliases={1: 0, 2: 1, 3: 2},
        compiler_params=pltpu.CompilerParams(vmem_limit_bytes=TRANSFORM_BYTES),
        cost_estimate=pl.CostEstimate(flops=5_000_000_000, bytes_accessed=3_000_000, transcendentals=0),
    )(*map(in_vmem, (t1, t2, t3, o, m1, m1r)))


def second_kernel(t2_ref, t3_ref, o_ref, m2_ref, m3_ref, a8_ref, d2_ref, two):
    for q in range(4):
        for slot in range(3):
            into = d2_ref if slot == 0 else two.at[slot - 1]
            into[q * 64 : (q + 1) * 64, :] = m2_ref[q, slot]
    t2 = t2_ref[...]
    x2 = dot(d2_ref[...], t2.astype(BF16)).astype(BF16)
    above = dot(two[...].reshape(512, 256), x2)
    t3 = t3_ref[...] - above[:256]
    o = o_ref[...] - above[256:]
    for k in range(8):
        cut = slice(k // 2 * 128, k // 2 * 128 + 128)
        odd = k % 2 == 1
        a8_ref[k, :256] = join_halves(t3[:, cut], o[:, cut], odd).astype(BF16)
        a8_ref[k, 256:384] = join_halves(t2[:128, cut], t2[128:, cut], odd).astype(BF16)
        for slot in range(2):
            for side in range(2):
                start = 384 + side * 64 + slot * 32
                a8_ref[k, start : start + 32] = m3_ref[:, slot, side * 128 : (side + 1) * 128]


def second_level(t2, t3, o, m2, m3):
    return pl.pallas_call(
        second_kernel,
        name="second",
        out_shape=[jax.ShapeDtypeStruct((8, 512, 128), BF16), pltpu.VMEM((256, 256), BF16)],
        scratch_shapes=[pltpu.VMEM((2, 256, 256), BF16)],
        compiler_params=pltpu.CompilerParams(vmem_limit_bytes=TRANSFORM_BYTES),
        cost_estimate=pl.CostEstimate(flops=200_000_000, bytes_accessed=3_000_000, transcendentals=0),
    )(*map(in_vmem, (t2, t3, o, m2, m3)))


def third_kernel(r8_ref, *rest):
    x3_ref, out_ref, own2_ref, sent2_ref, d3, l3, v = rest[-7:]
    total = r8_ref[0, :256].astype(F32)
    for k in range(1, 8):
        total = total + r8_ref[k, :256].astype(F32)
    for k in range(8):
        for side in range(2):
            cut = slice(side * 128, (side + 1) * 128)
            start = 384 + side * 64
            d3[k * 32 : (k + 1) * 32, cut] = r8_ref[k, start : start + 32]
            l3[k * 32 : (k + 1) * 32, cut] = r8_ref[k, start + 32 : start + 64]
    x3 = -dot_wide(d3[...], total)
    x3_ref[...] = jnp.transpose(x3)[:64, :].astype(BF16)
    v[...] = total + pltpu.roll(dot_wide(l3[...], x3), 64, 1)
    low = low_lanes((8, 128))
    for p in range(16):
        upper, lower = v[p * 16 : p * 16 + 8, :], v[p * 16 + 8 : p * 16 + 16, :]
        out_ref[p] = jnp.where(low, pltpu.roll(upper, 64, 1), lower).astype(BF16)
    sums = []
    for quad in range(2):
        folded = r8_ref[4 * quad, 256:384].astype(F32)
        for k in range(1, 4):
            folded = folded + r8_ref[4 * quad + k, 256:384].astype(F32)
        sums.append(folded)
    in_second = ((lax.axis_index("srow") >> 2) & 1) == 1
    own, other = jnp.where(in_second, sums[1], sums[0]), jnp.where(in_second, sums[0], sums[1])
    own2_ref[...] = own
    sent2_ref[...] = other.astype(BF16)


def third_level(r8, *after):
    return pl.pallas_call(
        third_kernel,
        name="third",
        in_specs=[pl.BlockSpec(memory_space=pltpu.VMEM)] + [pl.BlockSpec(memory_space=pl.ANY)] * len(after),
        out_shape=[
            jax.ShapeDtypeStruct((64, 256), BF16),
            pltpu.VMEM((16, 8, 128), BF16),
            pltpu.VMEM((128, 128), F32),
            pltpu.VMEM((128, 128), BF16),
        ],
        scratch_shapes=[pltpu.VMEM((256, 256), BF16), pltpu.VMEM((256, 256), BF16), pltpu.VMEM((256, 128), F32)],
        compiler_params=pltpu.CompilerParams(vmem_limit_bytes=SMALL_BYTES),
        cost_estimate=pl.CostEstimate(flops=70_000_000, bytes_accessed=1_300_000, transcendentals=0),
    )(in_vmem(r8), *after)


def lower_kernel(t1_ref, came1_ref, own2_ref, came2_ref, d1_ref, d2_ref, x1_ref, x2_ref):
    kept_one = jnp.concatenate([own_and_other(t1_ref, half)[0] for half in range(2)], axis=1)
    sum_one = kept_one + came1_ref[...].astype(F32)
    x1_ref[...] = (-dot_wide(d1_ref[...], sum_one)).astype(BF16)
    own, came = own2_ref[...], came2_ref[...].astype(F32)
    in_second = ((lax.axis_index("srow") >> 2) & 1) == 1
    first, second = jnp.where(in_second, came, own), jnp.where(in_second, own, came)
    sum_two = jnp.concatenate([join_halves(first, second, False), join_halves(first, second, True)], axis=0)
    x2_ref[...] = (-dot_wide(d2_ref[...], sum_two)).astype(BF16)


def lower_levels(t1, came1, own2, came2, d1, d2):
    return pl.pallas_call(
        lower_kernel,
        name="lower",
        out_shape=[jax.ShapeDtypeStruct((256, 256), BF16), jax.ShapeDtypeStruct((256, 128), BF16)],
        compiler_params=pltpu.CompilerParams(vmem_limit_bytes=SMALL_BYTES),
        cost_estimate=pl.CostEstimate(flops=1, bytes_accessed=1, transcendentals=0),
    )(*map(in_vmem, (t1, came1, own2, came2, d1, d2)))


def final_kernel(r_ref, after_ref, out_ref):
    total = r_ref[0].astype(F32)
    for k in range(1, 16):
        total = total + r_ref[k].astype(F32)
    out_ref[0:8, :] = total[:, :64]
    out_ref[8:16, :] = pltpu.roll(total, 64, 1)[:, :64]


def final_sum(received, after):
    return pl.pallas_call(
        final_kernel,
        name="final",
        in_specs=[pl.BlockSpec(memory_space=pltpu.VMEM), pl.BlockSpec(memory_space=pl.ANY)],
        out_shape=jax.ShapeDtypeStruct((16, 64), F32),
        compiler_params=pltpu.CompilerParams(vmem_limit_bytes=SMALL_BYTES),
        cost_estimate=pl.CostEstimate(flops=20_000, bytes_accessed=40_000, transcendentals=0),
    )(in_vmem(received), in_hbm(after))


def swap(block, flip):
    return lax.ppermute(block, "srow", [(i, i ^ flip) for i in range(32)])


def shards(
    leaf_rhs, leaf_inverse, leaf_blocks, leaf_outer, leaf_targets, level_one, level_two, level_three
):
    m1, m3 = level_one[:, 0], level_three[:, 0]
    m1r = swap(m1, 1)
    m2 = jnp.broadcast_to(jnp.transpose(level_two[:, 0], (1, 0, 2)), (4, 3, 64, 256))
    m2 = lax.all_to_all(m2, "srow", 0, 0, axis_index_groups=GROUPS_4, tiled=True)
    t1, t2, t3, o, sent1 = leaf_terms(
        leaf_targets[0, 0], leaf_inverse[0, 0], leaf_rhs[0, 0], leaf_blocks[0, 0], leaf_outer[0, 0]
    )
    came1 = swap(sent1, 1)
    t2, t3, o, d1 = first_level(t1, t2, t3, o, m1, m1r)
    a8, d2 = second_level(t2, t3, o, m2, m3)
    r8 = lax.all_to_all(a8, "srow", 0, 0, axis_index_groups=GROUPS_8, tiled=True)
    x3, parts, own2, sent2 = third_level(r8)
    received = lax.all_to_all(parts, "scol", 0, 0, tiled=True)
    x1, x2 = lower_levels(t1, came1, own2, swap(sent2, 4), d1, d2)
    outer_update = final_sum(received, x2)
    return (x1[:, None, :], x2[:, None, :], jnp.transpose(x3)[:, None, :], outer_update)


def solution(mesh):
    placed = (
        P("srow", "scol", None, None, None),
        P("srow", "scol", None, None, None),
        P("srow", "scol", None, None, None, None),
        P("srow", "scol", None, None, None),
        P("srow", "scol", None, None),
        P("srow", "scol", None, None),
        P("srow", "scol", None, None),
        P("srow", "scol", None, None),
    )
    return jax.shard_map(
        shards,
        mesh=mesh,
        in_specs=placed,
        out_specs=(
            P(None, "scol", "srow"),
            P(None, "scol", "srow"),
            P(None, "scol", "srow"),
            P("scol", "srow"),
        ),
        check_vma=False,
    )
```

```python
import jax
import jax.numpy as jnp
from jax import lax
from jax.experimental import pallas as pl
from jax.experimental.pallas import tpu as pltpu
from jax.sharding import PartitionSpec as P

F32 = jnp.float32
BF16 = jnp.bfloat16
LEAF_BYTES = 12 << 20
TRANSFORM_BYTES = 6 << 20
SMALL_BYTES = 4 << 20
GROUPS_8 = [[g * 8 + i for i in range(8)] for g in range(4)]
GROUPS_4 = [[g * 4 + i for i in range(4)] for g in range(8)]


def in_vmem(x):
    return pltpu.with_memory_space_constraint(x, pltpu.VMEM)


def in_hbm(x):
    return pltpu.with_memory_space_constraint(x, pltpu.HBM)


def dot(a, b):
    return jnp.dot(a, b, preferred_element_type=F32)


def dot_wide(a, b):
    high = b.astype(BF16)
    low = (b - high.astype(F32)).astype(BF16)
    return dot(a, high) + dot(a, low)


def low_lanes(shape):
    return lax.broadcasted_iota(jnp.int32, shape, 1) < 64


def join_halves(first, second, upper):
    low = low_lanes(first.shape)
    if upper:
        return jnp.where(low, pltpu.roll(first, 64, 1), second)
    return jnp.where(low, first, pltpu.roll(second, 64, 1))


def tile(ref, t):
    return ref[:, t * 128 : (t + 1) * 128]


def spread_kernel(x_ref, out_hbm, sems):
    copies = [pltpu.make_async_copy(x_ref, out_hbm.at[i], sems.at[i]) for i in range(4)]
    for copy in copies:
        copy.start()
    for copy in copies:
        copy.wait()


def spread(x):
    return pl.pallas_call(
        spread_kernel,
        name="spread",
        in_specs=[pl.BlockSpec(memory_space=pltpu.VMEM)],
        out_specs=pl.BlockSpec(memory_space=pl.ANY),
        out_shape=pltpu.HBM((4,) + x.shape, x.dtype),
        scratch_shapes=[pltpu.SemaphoreType.DMA((4,))],
        compiler_params=pltpu.CompilerParams(vmem_limit_bytes=1 << 20),
        cost_estimate=pl.CostEstimate(flops=1000, bytes_accessed=500_000, transcendentals=0),
    )(in_vmem(x))


def leaf_kernel(
    w_ref, inv_hbm, rhs_hbm, blk_hbm, out_hbm, m3_hbm,
    t1_ref, t2_ref, t3_ref, o_ref, sent_ref, a8_hbm,
    inv, rhs, blk, out, y, masked, m3, folded, sems, sends,
):
    copies = []
    for j in range(4):
        pairs = ((inv_hbm, inv), (rhs_hbm, rhs), (blk_hbm, blk), (out_hbm, out))
        copies.append([pltpu.make_async_copy(a.at[j], b.at[j], sems.at[j, i]) for i, (a, b) in enumerate(pairs)])
    third = pltpu.make_async_copy(m3_hbm, m3, sems.at[0, 4])
    third.start()
    for first in (0, 2):
        for j in range(4):
            for copy in copies[j][first : first + 2]:
                copy.start()
    third.wait()
    for slot in range(2):
        for side in range(2):
            start = side * 64 + slot * 32
            folded[start : start + 32] = m3[:, slot, side * 128 : (side + 1) * 128]
    blocks = [pltpu.make_async_copy(folded, a8_hbm.at[k, 256:384], sends.at[k]) for k in range(8)]
    for copy in blocks:
        copy.start()
    for j in range(4):
        copies[j][0].wait()
        copies[j][1].wait()
        y[j * 256 : (j + 1) * 256, :] = dot(inv[j], rhs[j]).astype(BF16)
    for j in range(4):
        copies[j][2].wait()
        copies[j][3].wait()
        for t in range(4):
            block = blk[j, t] if t < 3 else out[j]
            masked[t, :, j * 256 : (j + 1) * 256] = block * w_ref[j, t].astype(F32).astype(BF16)
    for t, into in enumerate((t1_ref, t2_ref, t3_ref, o_ref)):
        into[...] = dot(masked[t], y[...]).astype(into.dtype)
    for half in range(2):
        sent_ref[:, half * 128 : (half + 1) * 128] = own_and_other(t1_ref, half)[1].astype(BF16)
    for copy in blocks:
        copy.wait()


def own_and_other(t1_ref, half):
    first, second = tile(t1_ref, 2 * half).astype(F32), tile(t1_ref, 2 * half + 1).astype(F32)
    even = join_halves(first, second, False)
    odd = join_halves(first, second, True)
    own_upper = (lax.axis_index("srow") & 1) == 1
    return jnp.where(own_upper, odd, even), jnp.where(own_upper, even, odd)


def leaf_terms(weights, inverse, rhs, blocks, outer, m3):
    full = pltpu.VMEM((256, 512), F32)
    return pl.pallas_call(
        leaf_kernel,
        name="leaf",
        in_specs=[pl.BlockSpec(memory_space=pltpu.SMEM)] + [pl.BlockSpec(memory_space=pl.ANY)] * 5,
        out_specs=[pl.BlockSpec(memory_space=pltpu.VMEM)] * 5 + [pl.BlockSpec(memory_space=pl.ANY)],
        out_shape=[
            pltpu.VMEM((256, 512), BF16), full, full, full, pltpu.VMEM((256, 256), BF16),
            pltpu.HBM((8, 384, 128), BF16),
        ],
        scratch_shapes=[
            pltpu.VMEM((4, 256, 256), BF16),
            pltpu.VMEM((4, 256, 512), BF16),
            pltpu.VMEM((4, 3, 256, 256), BF16),
            pltpu.VMEM((4, 256, 256), BF16),
            pltpu.VMEM((1024, 512), BF16),
            pltpu.VMEM((4, 256, 1024), BF16),
            pltpu.VMEM((32, 2, 256), BF16),
            pltpu.VMEM((128, 128), BF16),
            pltpu.SemaphoreType.DMA((4, 5)),
            pltpu.SemaphoreType.DMA((8,)),
        ],
        compiler_params=pltpu.CompilerParams(vmem_limit_bytes=LEAF_BYTES),
        cost_estimate=pl.CostEstimate(flops=1_342_177_280, bytes_accessed=6_000_000, transcendentals=0),
    )(*map(in_hbm, (weights, inverse, rhs, blocks, outer, m3)))


def first_kernel(t1_ref, t2_ref, t3_ref, o_ref, m1_ref, m1r_ref, t2n_ref, t3n_ref, on_ref, d1_ref, sent_ref, kept_ref, one, shares):
    row = lax.axis_index("srow")
    own = pl.multiple_of((row & 1) * 128, 128)
    other = pl.multiple_of(128 - (row & 1) * 128, 128)
    for slot in range(4):
        into = d1_ref if slot == 0 else one.at[slot - 1]
        into[pl.ds(own, 128), :] = m1_ref[:, slot, :]
        into[pl.ds(other, 128), :] = m1r_ref[:, slot, :]
    x1 = dot(d1_ref[...], t1_ref[...]).astype(BF16)
    under = dot(one[...].reshape(768, 256), x1)
    t2 = t2_ref[...] - under[:256]
    t2n_ref[...] = t2
    for t in range(2):
        first, second = t2[:, t * 128 : (t + 1) * 128], t2[:, (t + 2) * 128 : (t + 3) * 128]
        shares[2 * t] = join_halves(first, second, False)
        shares[2 * t + 1] = join_halves(first, second, True)
    place = row & 3
    for i in range(2):
        kept_ref[i] = shares[place ^ i].astype(BF16)
        sent_ref[i] = shares[place ^ 3 ^ i].astype(BF16)
    t3n_ref[...] = t3_ref[...] - under[256:512]
    on_ref[...] = o_ref[...] - under[512:]


def first_level(t1, t2, t3, o, m1, m1r):
    full = pltpu.VMEM((256, 512), F32)
    two = pltpu.VMEM((2, 256, 128), BF16)
    return pl.pallas_call(
        first_kernel,
        name="first",
        out_shape=[full, full, full, pltpu.VMEM((256, 256), BF16), two, two],
        scratch_shapes=[pltpu.VMEM((3, 256, 256), BF16), pltpu.VMEM((4, 256, 128), F32)],
        input_output_aliases={1: 0, 2: 1, 3: 2},
        compiler_params=pltpu.CompilerParams(vmem_limit_bytes=TRANSFORM_BYTES),
        cost_estimate=pl.CostEstimate(flops=5_000_000_000, bytes_accessed=3_000_000, transcendentals=0),
    )(*map(in_vmem, (t1, t2, t3, o, m1, m1r)))


def second_kernel(t2_ref, t3_ref, o_ref, m2_ref, blocks_ref, a8_hbm, d2_ref, two, a8, sems):
    for q in range(4):
        for slot in range(3):
            into = d2_ref if slot == 0 else two.at[slot - 1]
            into[q * 64 : (q + 1) * 64, :] = m2_ref[q, slot]
    x2 = dot(d2_ref[...], t2_ref[...].astype(BF16)).astype(BF16)
    copies = []
    for half in range(2):
        wide = slice(half * 256, half * 256 + 256)
        above = dot(two[...].reshape(512, 256), x2[:, wide])
        t3 = t3_ref[:, wide] - above[:256]
        o = o_ref[:, wide] - above[256:]
        for i in range(4):
            k = half * 4 + i
            cut = slice(i // 2 * 128, i // 2 * 128 + 128)
            a8[k] = join_halves(t3[:, cut], o[:, cut], i % 2 == 1).astype(BF16)
            copies.append(pltpu.make_async_copy(a8.at[k], a8_hbm.at[k, :256], sems.at[k]))
            copies[-1].start()
    for copy in copies:
        copy.wait()


def second_level(t2, t3, o, m2, blocks):
    return pl.pallas_call(
        second_kernel,
        name="second",
        in_specs=[pl.BlockSpec(memory_space=pltpu.VMEM)] * 4 + [pl.BlockSpec(memory_space=pl.ANY)],
        out_specs=[pl.BlockSpec(memory_space=pl.ANY), pl.BlockSpec(memory_space=pltpu.VMEM)],
        out_shape=[pltpu.HBM((8, 384, 128), BF16), pltpu.VMEM((256, 256), BF16)],
        scratch_shapes=[
            pltpu.VMEM((2, 256, 256), BF16),
            pltpu.VMEM((8, 256, 128), BF16),
            pltpu.SemaphoreType.DMA((8,)),
        ],
        input_output_aliases={4: 0},
        compiler_params=pltpu.CompilerParams(vmem_limit_bytes=TRANSFORM_BYTES),
        cost_estimate=pl.CostEstimate(flops=200_000_000, bytes_accessed=3_000_000, transcendentals=0),
    )(*map(in_vmem, (t2, t3, o, m2)), in_hbm(blocks))


def third_kernel(r8_ref, x3_ref, out_ref, d3, l3, v):
    total = r8_ref[0, :256].astype(F32)
    for k in range(1, 8):
        total = total + r8_ref[k, :256].astype(F32)
    for k in range(8):
        for side in range(2):
            cut = slice(side * 128, (side + 1) * 128)
            start = 256 + side * 64
            d3[k * 32 : (k + 1) * 32, cut] = r8_ref[k, start : start + 32]
            l3[k * 32 : (k + 1) * 32, cut] = r8_ref[k, start + 32 : start + 64]
    x3 = -dot_wide(d3[...], total)
    x3_ref[...] = jnp.transpose(x3)[:64, :].astype(BF16)
    v[...] = total + pltpu.roll(dot_wide(l3[...], x3), 64, 1)
    low = low_lanes((8, 128))
    for p in range(16):
        upper, lower = v[p * 16 : p * 16 + 8, :], v[p * 16 + 8 : p * 16 + 16, :]
        out_ref[p] = jnp.where(low, pltpu.roll(upper, 64, 1), lower)


def middle_kernel(kept_ref, came_ref, own_ref, sent_ref):
    own_ref[...] = kept_ref[0].astype(F32) + came_ref[0].astype(F32)
    sent_ref[...] = (kept_ref[1].astype(F32) + came_ref[1].astype(F32)).astype(BF16)


def middle_sums(kept, came):
    return pl.pallas_call(
        middle_kernel,
        name="middle",
        out_shape=[pltpu.VMEM((256, 128), F32), pltpu.VMEM((256, 128), BF16)],
        compiler_params=pltpu.CompilerParams(vmem_limit_bytes=SMALL_BYTES),
        cost_estimate=pl.CostEstimate(flops=1, bytes_accessed=1, transcendentals=0),
    )(in_vmem(kept), in_vmem(came))


def third_level(r8):
    return pl.pallas_call(
        third_kernel,
        name="third",
        out_shape=[
            jax.ShapeDtypeStruct((64, 256), BF16),
            pltpu.VMEM((16, 8, 128), F32),
        ],
        scratch_shapes=[pltpu.VMEM((256, 256), BF16), pltpu.VMEM((256, 256), BF16), pltpu.VMEM((256, 128), F32)],
        compiler_params=pltpu.CompilerParams(vmem_limit_bytes=SMALL_BYTES),
        cost_estimate=pl.CostEstimate(flops=70_000_000, bytes_accessed=1_300_000, transcendentals=0),
    )(in_vmem(r8))


def lower_kernel(t1_ref, came1_ref, own2_ref, came2_ref, d1_ref, d2_ref, x1_ref, x2_ref):
    kept_one = jnp.concatenate([own_and_other(t1_ref, half)[0] for half in range(2)], axis=1)
    sum_one = kept_one + came1_ref[...].astype(F32)
    x1_ref[...] = (-dot_wide(d1_ref[...], sum_one)).astype(BF16)
    x2_ref[...] = (-dot_wide(d2_ref[...], own2_ref[...] + came2_ref[...].astype(F32))).astype(BF16)


def lower_levels(t1, came1, own2, came2, d1, d2):
    return pl.pallas_call(
        lower_kernel,
        name="lower",
        out_shape=[jax.ShapeDtypeStruct((256, 256), BF16), jax.ShapeDtypeStruct((256, 128), BF16)],
        compiler_params=pltpu.CompilerParams(vmem_limit_bytes=SMALL_BYTES),
        cost_estimate=pl.CostEstimate(flops=1, bytes_accessed=1, transcendentals=0),
    )(*map(in_vmem, (t1, came1, own2, came2, d1, d2)))


def final_kernel(r_ref, after_ref, out_ref):
    total = r_ref[0]
    for k in range(1, 16):
        total = total + r_ref[k]
    out_ref[0:8, :] = total[:, :64]
    out_ref[8:16, :] = pltpu.roll(total, 64, 1)[:, :64]


def final_sum(received, after):
    return pl.pallas_call(
        final_kernel,
        name="final",
        in_specs=[pl.BlockSpec(memory_space=pltpu.VMEM), pl.BlockSpec(memory_space=pl.ANY)],
        out_shape=jax.ShapeDtypeStruct((16, 64), F32),
        compiler_params=pltpu.CompilerParams(vmem_limit_bytes=SMALL_BYTES),
        cost_estimate=pl.CostEstimate(flops=20_000, bytes_accessed=40_000, transcendentals=0),
    )(in_vmem(received), in_hbm(after))


def swap(block, flip):
    return lax.ppermute(block, "srow", [(i, i ^ flip) for i in range(32)])


def shards(
    leaf_rhs, leaf_inverse, leaf_blocks, leaf_outer, leaf_targets, level_one, level_two, level_three
):
    m1, m3 = level_one[:, 0], level_three[:, 0]
    m1r = swap(m1, 1)
    m2 = spread(jnp.transpose(level_two[:, 0], (1, 0, 2)))
    m2 = lax.all_to_all(m2, "srow", 0, 0, axis_index_groups=GROUPS_4, tiled=True)
    t1, t2, t3, o, sent1, a8 = leaf_terms(
        leaf_targets[0, 0], leaf_inverse[0, 0], leaf_rhs[0, 0], leaf_blocks[0, 0], leaf_outer[0, 0], m3
    )
    came1 = swap(sent1, 1)
    t2, t3, o, d1, sent2, kept2 = first_level(t1, t2, t3, o, m1, m1r)
    a8, d2 = second_level(t2, t3, o, m2, a8)
    r8 = lax.all_to_all(a8, "srow", 0, 0, axis_index_groups=GROUPS_8, tiled=True)
    x3, parts = third_level(r8)
    own2, sent2 = middle_sums(kept2, swap(sent2, 3))
    received = lax.all_to_all(parts, "scol", 0, 0, tiled=True)
    x1, x2 = lower_levels(t1, came1, own2, swap(sent2, 1), d1, d2)
    outer_update = final_sum(received, x2)
    return (x1[:, None, :], x2[:, None, :], jnp.transpose(x3)[:, None, :], outer_update)


def solution(mesh):
    placed = (
        P("srow", "scol", None, None, None),
        P("srow", "scol", None, None, None),
        P("srow", "scol", None, None, None, None),
        P("srow", "scol", None, None, None),
        P("srow", "scol", None, None),
        P("srow", "scol", None, None),
        P("srow", "scol", None, None),
        P("srow", "scol", None, None),
    )
    return jax.shard_map(
        shards,
        mesh=mesh,
        in_specs=placed,
        out_specs=(
            P(None, "scol", "srow"),
            P(None, "scol", "srow"),
            P(None, "scol", "srow"),
            P("scol", "srow"),
        ),
        check_vma=False,
    )
```

```python
import jax
import jax.numpy as jnp
from jax import lax
from jax.experimental import pallas as pl
from jax.experimental.pallas import tpu as pltpu
from jax.sharding import PartitionSpec as P

F32 = jnp.float32
BF16 = jnp.bfloat16
LEAF_BYTES = 12 << 20
TRANSFORM_BYTES = 6 << 20
SMALL_BYTES = 4 << 20
GROUPS_8 = [[g * 8 + i for i in range(8)] for g in range(4)]
GROUPS_4 = [[g * 4 + i for i in range(4)] for g in range(8)]


def in_vmem(x):
    return pltpu.with_memory_space_constraint(x, pltpu.VMEM)


def in_hbm(x):
    return pltpu.with_memory_space_constraint(x, pltpu.HBM)


def dot(a, b):
    return jnp.dot(a, b, preferred_element_type=F32)


def dot_wide(a, b):
    high = b.astype(BF16)
    low = (b - high.astype(F32)).astype(BF16)
    return dot(a, high) + dot(a, low)


def low_lanes(shape):
    return lax.broadcasted_iota(jnp.int32, shape, 1) < 64


def join_halves(first, second, upper):
    low = low_lanes(first.shape)
    if upper:
        return jnp.where(low, pltpu.roll(first, 64, 1), second)
    return jnp.where(low, first, pltpu.roll(second, 64, 1))


def tile(ref, t):
    return ref[:, t * 128 : (t + 1) * 128]


def spread_kernel(x_ref, out_hbm, sems):
    copies = [pltpu.make_async_copy(x_ref, out_hbm.at[i], sems.at[i]) for i in range(4)]
    for copy in copies:
        copy.start()
    for copy in copies:
        copy.wait()


def spread(x):
    return pl.pallas_call(
        spread_kernel,
        name="spread",
        in_specs=[pl.BlockSpec(memory_space=pltpu.VMEM)],
        out_specs=pl.BlockSpec(memory_space=pl.ANY),
        out_shape=pltpu.HBM((4,) + x.shape, x.dtype),
        scratch_shapes=[pltpu.SemaphoreType.DMA((4,))],
        compiler_params=pltpu.CompilerParams(vmem_limit_bytes=1 << 20),
        cost_estimate=pl.CostEstimate(flops=1000, bytes_accessed=500_000, transcendentals=0),
    )(in_vmem(x))


def leaf_kernel(
    w_ref, inv_hbm, rhs_hbm, blk_hbm, out_hbm, m3_hbm,
    t1_ref, t2_ref, t3_ref, o_ref, a8_hbm,
    inv, rhs, blk, out, y, masked, m3, folded, sems, sends,
):
    copies = []
    for j in range(4):
        pairs = ((inv_hbm, inv), (rhs_hbm, rhs), (blk_hbm, blk), (out_hbm, out))
        copies.append([pltpu.make_async_copy(a.at[j], b.at[j], sems.at[j, i]) for i, (a, b) in enumerate(pairs)])
    third = pltpu.make_async_copy(m3_hbm, m3, sems.at[0, 4])
    third.start()
    for first in (0, 2):
        for j in range(4):
            for copy in copies[j][first : first + 2]:
                copy.start()
    third.wait()
    for slot in range(2):
        for side in range(2):
            start = side * 64 + slot * 32
            folded[start : start + 32] = m3[:, slot, side * 128 : (side + 1) * 128]
    blocks = [pltpu.make_async_copy(folded, a8_hbm.at[k, 256:384], sends.at[k]) for k in range(8)]
    for copy in blocks:
        copy.start()
    for j in range(4):
        copies[j][0].wait()
        copies[j][1].wait()
        y[j * 256 : (j + 1) * 256, :] = dot(inv[j], rhs[j]).astype(BF16)
    for j in range(4):
        copies[j][2].wait()
        copies[j][3].wait()
        for t in range(4):
            block = blk[j, t] if t < 3 else out[j]
            masked[t, :, j * 256 : (j + 1) * 256] = block * w_ref[j, t].astype(F32).astype(BF16)
    for t, into in enumerate((t1_ref, t2_ref, t3_ref, o_ref)):
        into[...] = dot(masked[t], y[...]).astype(into.dtype)
    for copy in blocks:
        copy.wait()


def own_and_other(t1_ref, half):
    first, second = tile(t1_ref, 2 * half).astype(F32), tile(t1_ref, 2 * half + 1).astype(F32)
    even = join_halves(first, second, False)
    odd = join_halves(first, second, True)
    own_upper = (lax.axis_index("srow") & 1) == 1
    return jnp.where(own_upper, odd, even), jnp.where(own_upper, even, odd)


def leaf_terms(weights, inverse, rhs, blocks, outer, m3):
    full = pltpu.VMEM((256, 512), F32)
    return pl.pallas_call(
        leaf_kernel,
        name="leaf",
        in_specs=[pl.BlockSpec(memory_space=pltpu.SMEM)] + [pl.BlockSpec(memory_space=pl.ANY)] * 5,
        out_specs=[pl.BlockSpec(memory_space=pltpu.VMEM)] * 4 + [pl.BlockSpec(memory_space=pl.ANY)],
        out_shape=[
            pltpu.VMEM((256, 512), BF16), full, full, full,
            pltpu.HBM((8, 384, 128), BF16),
        ],
        scratch_shapes=[
            pltpu.VMEM((4, 256, 256), BF16),
            pltpu.VMEM((4, 256, 512), BF16),
            pltpu.VMEM((4, 3, 256, 256), BF16),
            pltpu.VMEM((4, 256, 256), BF16),
            pltpu.VMEM((1024, 512), BF16),
            pltpu.VMEM((4, 256, 1024), BF16),
            pltpu.VMEM((32, 2, 256), BF16),
            pltpu.VMEM((128, 128), BF16),
            pltpu.SemaphoreType.DMA((4, 5)),
            pltpu.SemaphoreType.DMA((8,)),
        ],
        compiler_params=pltpu.CompilerParams(vmem_limit_bytes=LEAF_BYTES),
        cost_estimate=pl.CostEstimate(flops=1_342_177_280, bytes_accessed=6_000_000, transcendentals=0),
    )(*map(in_hbm, (weights, inverse, rhs, blocks, outer, m3)))


def first_kernel(t1_ref, t2_ref, t3_ref, o_ref, m1_ref, m1r_ref, t2n_ref, t3n_ref, on_ref, d1_ref, kept_ref, near_ref, far_ref, ring_ref, one, shares):
    row = lax.axis_index("srow")
    own = pl.multiple_of((row & 1) * 128, 128)
    other = pl.multiple_of(128 - (row & 1) * 128, 128)
    for slot in range(4):
        into = d1_ref if slot == 0 else one.at[slot - 1]
        into[pl.ds(own, 128), :] = m1_ref[:, slot, :]
        into[pl.ds(other, 128), :] = m1r_ref[:, slot, :]
    x1 = dot(d1_ref[...], t1_ref[...]).astype(BF16)
    under = dot(one[...].reshape(768, 256), x1)
    t2 = t2_ref[...] - under[:256]
    t2n_ref[...] = t2
    for t in range(2):
        first, second = t2[:, t * 128 : (t + 1) * 128], t2[:, (t + 2) * 128 : (t + 3) * 128]
        shares[2 * t] = join_halves(first, second, False)
        shares[2 * t + 1] = join_halves(first, second, True)
    place = row & 3
    for half in range(2):
        near_ref[:, half * 128 : (half + 1) * 128] = own_and_other(t1_ref, half)[1].astype(BF16)
    near_ref[:, 256:] = shares[place ^ 1].astype(BF16)
    kept_ref[...] = shares[place]
    far_ref[...] = shares[place ^ 2].astype(BF16)
    ring_ref[...] = shares[place ^ 3].astype(BF16)
    t3n_ref[...] = t3_ref[...] - under[256:512]
    on_ref[...] = o_ref[...] - under[512:]


def first_level(t1, t2, t3, o, m1, m1r):
    full = pltpu.VMEM((256, 512), F32)
    share = pltpu.VMEM((256, 128), BF16)
    return pl.pallas_call(
        first_kernel,
        name="first",
        out_shape=[
            full, full, full, pltpu.VMEM((256, 256), BF16),
            pltpu.VMEM((256, 128), F32), pltpu.VMEM((256, 384), BF16), share, share,
        ],
        scratch_shapes=[pltpu.VMEM((3, 256, 256), BF16), pltpu.VMEM((4, 256, 128), F32)],
        input_output_aliases={1: 0, 2: 1, 3: 2},
        compiler_params=pltpu.CompilerParams(vmem_limit_bytes=TRANSFORM_BYTES),
        cost_estimate=pl.CostEstimate(flops=5_000_000_000, bytes_accessed=3_000_000, transcendentals=0),
    )(*map(in_vmem, (t1, t2, t3, o, m1, m1r)))


def second_kernel(t2_ref, t3_ref, o_ref, m2_ref, blocks_ref, a8_hbm, d2_ref, two, a8, sems):
    for q in range(4):
        for slot in range(3):
            into = d2_ref if slot == 0 else two.at[slot - 1]
            into[q * 64 : (q + 1) * 64, :] = m2_ref[q, slot]
    x2 = dot(d2_ref[...], t2_ref[...].astype(BF16)).astype(BF16)
    copies = []
    for half in range(2):
        wide = slice(half * 256, half * 256 + 256)
        above = dot(two[...].reshape(512, 256), x2[:, wide])
        t3 = t3_ref[:, wide] - above[:256]
        o = o_ref[:, wide] - above[256:]
        for i in range(4):
            k = half * 4 + i
            cut = slice(i // 2 * 128, i // 2 * 128 + 128)
            a8[k] = join_halves(t3[:, cut], o[:, cut], i % 2 == 1).astype(BF16)
            copies.append(pltpu.make_async_copy(a8.at[k], a8_hbm.at[k, :256], sems.at[k]))
            copies[-1].start()
    for copy in copies:
        copy.wait()


def second_level(t2, t3, o, m2, blocks):
    return pl.pallas_call(
        second_kernel,
        name="second",
        in_specs=[pl.BlockSpec(memory_space=pltpu.VMEM)] * 4 + [pl.BlockSpec(memory_space=pl.ANY)],
        out_specs=[pl.BlockSpec(memory_space=pl.ANY), pl.BlockSpec(memory_space=pltpu.VMEM)],
        out_shape=[pltpu.HBM((8, 384, 128), BF16), pltpu.VMEM((256, 256), BF16)],
        scratch_shapes=[
            pltpu.VMEM((2, 256, 256), BF16),
            pltpu.VMEM((8, 256, 128), BF16),
            pltpu.SemaphoreType.DMA((8,)),
        ],
        input_output_aliases={4: 0},
        compiler_params=pltpu.CompilerParams(vmem_limit_bytes=TRANSFORM_BYTES),
        cost_estimate=pl.CostEstimate(flops=200_000_000, bytes_accessed=3_000_000, transcendentals=0),
    )(*map(in_vmem, (t2, t3, o, m2)), in_hbm(blocks))


def third_kernel(r8_ref, x3_ref, out_ref, d3, l3, v):
    total = r8_ref[0, :256].astype(F32)
    for k in range(1, 8):
        total = total + r8_ref[k, :256].astype(F32)
    for k in range(8):
        for side in range(2):
            cut = slice(side * 128, (side + 1) * 128)
            start = 256 + side * 64
            d3[k * 32 : (k + 1) * 32, cut] = r8_ref[k, start : start + 32]
            l3[k * 32 : (k + 1) * 32, cut] = r8_ref[k, start + 32 : start + 64]
    x3 = -dot_wide(d3[...], total)
    x3_ref[...] = jnp.transpose(x3)[:64, :].astype(BF16)
    v[...] = total + pltpu.roll(dot_wide(l3[...], x3), 64, 1)
    low = low_lanes((8, 128))
    for p in range(16):
        upper, lower = v[p * 16 : p * 16 + 8, :], v[p * 16 + 8 : p * 16 + 16, :]
        out_ref[p] = jnp.where(low, pltpu.roll(upper, 64, 1), lower).astype(BF16)


def third_level(r8):
    return pl.pallas_call(
        third_kernel,
        name="third",
        out_shape=[
            jax.ShapeDtypeStruct((64, 256), BF16),
            pltpu.VMEM((16, 8, 128), BF16),
        ],
        scratch_shapes=[pltpu.VMEM((256, 256), BF16), pltpu.VMEM((256, 256), BF16), pltpu.VMEM((256, 128), F32)],
        compiler_params=pltpu.CompilerParams(vmem_limit_bytes=SMALL_BYTES),
        cost_estimate=pl.CostEstimate(flops=70_000_000, bytes_accessed=1, transcendentals=0),
    )(in_vmem(r8))


def lower_kernel(t1_ref, kept_ref, near_ref, far_ref, ring_ref, d1_ref, d2_ref, x1_ref, x2_ref):
    kept_one = jnp.concatenate([own_and_other(t1_ref, half)[0] for half in range(2)], axis=1)
    x1_ref[...] = (-dot_wide(d1_ref[...], kept_one + near_ref[:, :256].astype(F32))).astype(BF16)
    sum_two = kept_ref[...] + near_ref[:, 256:].astype(F32)
    sum_two = sum_two + far_ref[...].astype(F32) + ring_ref[...].astype(F32)
    x2_ref[...] = (-dot_wide(d2_ref[...], sum_two)).astype(BF16)


def lower_levels(t1, kept, near, far, ring, d1, d2):
    return pl.pallas_call(
        lower_kernel,
        name="lower",
        out_shape=[jax.ShapeDtypeStruct((256, 256), BF16), jax.ShapeDtypeStruct((256, 128), BF16)],
        compiler_params=pltpu.CompilerParams(vmem_limit_bytes=SMALL_BYTES),
        cost_estimate=pl.CostEstimate(flops=1, bytes_accessed=1, transcendentals=0),
    )(*map(in_vmem, (t1, kept, near, far, ring, d1, d2)))


def final_kernel(r_ref, after_ref, out_ref):
    total = r_ref[0].astype(F32)
    for k in range(1, 16):
        total = total + r_ref[k].astype(F32)
    out_ref[0:8, :] = total[:, :64]
    out_ref[8:16, :] = pltpu.roll(total, 64, 1)[:, :64]


def final_sum(received, after):
    return pl.pallas_call(
        final_kernel,
        name="final",
        in_specs=[pl.BlockSpec(memory_space=pltpu.VMEM), pl.BlockSpec(memory_space=pl.ANY)],
        out_shape=jax.ShapeDtypeStruct((16, 64), F32),
        compiler_params=pltpu.CompilerParams(vmem_limit_bytes=SMALL_BYTES),
        cost_estimate=pl.CostEstimate(flops=20_000, bytes_accessed=40_000, transcendentals=0),
    )(in_vmem(received), in_hbm(after))


def swap(block, flip):
    return lax.ppermute(block, "srow", [(i, i ^ flip) for i in range(32)])


def shards(
    leaf_rhs, leaf_inverse, leaf_blocks, leaf_outer, leaf_targets, level_one, level_two, level_three
):
    m1, m3 = level_one[:, 0], level_three[:, 0]
    m1r = swap(m1, 1)
    m2 = spread(jnp.transpose(level_two[:, 0], (1, 0, 2)))
    m2 = lax.all_to_all(m2, "srow", 0, 0, axis_index_groups=GROUPS_4, tiled=True)
    t1, t2, t3, o, a8 = leaf_terms(
        leaf_targets[0, 0], leaf_inverse[0, 0], leaf_rhs[0, 0], leaf_blocks[0, 0], leaf_outer[0, 0], m3
    )
    t2, t3, o, d1, kept, near, far, ring = first_level(t1, t2, t3, o, m1, m1r)
    a8, d2 = second_level(t2, t3, o, m2, a8)
    r8 = lax.all_to_all(a8, "srow", 0, 0, axis_index_groups=GROUPS_8, tiled=True)
    x3, parts = third_level(r8)
    received = lax.all_to_all(parts, "scol", 0, 0, tiled=True)
    x1, x2 = lower_levels(t1, kept, swap(near, 1), swap(far, 2), swap(ring, 3), d1, d2)
    outer_update = final_sum(received, x2)
    return (x1[:, None, :], x2[:, None, :], jnp.transpose(x3)[:, None, :], outer_update)


def solution(mesh):
    placed = (
        P("srow", "scol", None, None, None),
        P("srow", "scol", None, None, None),
        P("srow", "scol", None, None, None, None),
        P("srow", "scol", None, None, None),
        P("srow", "scol", None, None),
        P("srow", "scol", None, None),
        P("srow", "scol", None, None),
        P("srow", "scol", None, None),
    )
    return jax.shard_map(
        shards,
        mesh=mesh,
        in_specs=placed,
        out_specs=(
            P(None, "scol", "srow"),
            P(None, "scol", "srow"),
            P(None, "scol", "srow"),
            P("scol", "srow"),
        ),
        check_vma=False,
    )
```

```python
import jax
import jax.numpy as jnp
from jax import lax
from jax.experimental import pallas as pl
from jax.experimental.pallas import tpu as pltpu
from jax.sharding import PartitionSpec as P

F32 = jnp.float32
BF16 = jnp.bfloat16
LEAF_BYTES = 12 << 20
TRANSFORM_BYTES = 6 << 20
SMALL_BYTES = 4 << 20
GROUPS_8 = [[g * 8 + i for i in range(8)] for g in range(4)]
GROUPS_4 = [[g * 4 + i for i in range(4)] for g in range(8)]


def in_vmem(x):
    return pltpu.with_memory_space_constraint(x, pltpu.VMEM)


def in_hbm(x):
    return pltpu.with_memory_space_constraint(x, pltpu.HBM)


def dot(a, b):
    return jnp.dot(a, b, preferred_element_type=F32)


def dot_wide(a, b):
    high = b.astype(BF16)
    low = (b - high.astype(F32)).astype(BF16)
    return dot(a, high) + dot(a, low)


def low_lanes(shape):
    return lax.broadcasted_iota(jnp.int32, shape, 1) < 64


def join_halves(first, second, upper):
    low = low_lanes(first.shape)
    if upper:
        return jnp.where(low, pltpu.roll(first, 64, 1), second)
    return jnp.where(low, first, pltpu.roll(second, 64, 1))


def tile(ref, t):
    return ref[:, t * 128 : (t + 1) * 128]


def spread_kernel(x_ref, out_hbm, sems):
    copies = [pltpu.make_async_copy(x_ref, out_hbm.at[i], sems.at[i]) for i in range(4)]
    for copy in copies:
        copy.start()
    for copy in copies:
        copy.wait()


def spread(x):
    return pl.pallas_call(
        spread_kernel,
        name="spread",
        in_specs=[pl.BlockSpec(memory_space=pltpu.VMEM)],
        out_specs=pl.BlockSpec(memory_space=pl.ANY),
        out_shape=pltpu.HBM((4,) + x.shape, x.dtype),
        scratch_shapes=[pltpu.SemaphoreType.DMA((4,))],
        compiler_params=pltpu.CompilerParams(vmem_limit_bytes=1 << 20),
        cost_estimate=pl.CostEstimate(flops=1000, bytes_accessed=500_000, transcendentals=0),
    )(in_vmem(x))


def leaf_kernel(
    w_ref, inv_hbm, rhs_hbm, blk_hbm, out_hbm, m3_hbm,
    t1_ref, t2_ref, t3_ref, o_ref, a8_hbm,
    inv, rhs, blk, out, y, masked, m3, folded, sems, sends,
):
    copies = []
    for j in range(4):
        pairs = ((inv_hbm, inv), (rhs_hbm, rhs), (blk_hbm, blk), (out_hbm, out))
        copies.append([pltpu.make_async_copy(a.at[j], b.at[j], sems.at[j, i]) for i, (a, b) in enumerate(pairs)])
    third = pltpu.make_async_copy(m3_hbm, m3, sems.at[0, 4])
    third.start()
    for first in (0, 2):
        for j in range(4):
            for copy in copies[j][first : first + 2]:
                copy.start()
    third.wait()
    for slot in range(2):
        for side in range(2):
            start = side * 64 + slot * 32
            folded[start : start + 32] = m3[:, slot, side * 128 : (side + 1) * 128]
    blocks = [pltpu.make_async_copy(folded, a8_hbm.at[k, 256:384], sends.at[k]) for k in range(8)]
    for copy in blocks:
        copy.start()
    for j in range(4):
        copies[j][0].wait()
        copies[j][1].wait()
        y[j * 256 : (j + 1) * 256, :] = dot(inv[j], rhs[j]).astype(BF16)
    for j in range(4):
        copies[j][2].wait()
        copies[j][3].wait()
        for t in range(4):
            block = blk[j, t] if t < 3 else out[j]
            masked[t, :, j * 256 : (j + 1) * 256] = block * w_ref[j, t].astype(F32).astype(BF16)
    for t, into in enumerate((t1_ref, t2_ref, t3_ref, o_ref)):
        into[...] = dot(masked[t], y[...]).astype(into.dtype)
    for copy in blocks:
        copy.wait()


def own_and_other(t1_ref, half):
    first, second = tile(t1_ref, 2 * half).astype(F32), tile(t1_ref, 2 * half + 1).astype(F32)
    even = join_halves(first, second, False)
    odd = join_halves(first, second, True)
    own_upper = (lax.axis_index("srow") & 1) == 1
    return jnp.where(own_upper, odd, even), jnp.where(own_upper, even, odd)


def leaf_terms(weights, inverse, rhs, blocks, outer, m3):
    full = pltpu.VMEM((256, 512), F32)
    return pl.pallas_call(
        leaf_kernel,
        name="leaf",
        in_specs=[pl.BlockSpec(memory_space=pltpu.SMEM)] + [pl.BlockSpec(memory_space=pl.ANY)] * 5,
        out_specs=[pl.BlockSpec(memory_space=pltpu.VMEM)] * 4 + [pl.BlockSpec(memory_space=pl.ANY)],
        out_shape=[
            pltpu.VMEM((256, 512), BF16), full, full, full,
            pltpu.HBM((8, 384, 128), BF16),
        ],
        scratch_shapes=[
            pltpu.VMEM((4, 256, 256), BF16),
            pltpu.VMEM((4, 256, 512), BF16),
            pltpu.VMEM((4, 3, 256, 256), BF16),
            pltpu.VMEM((4, 256, 256), BF16),
            pltpu.VMEM((1024, 512), BF16),
            pltpu.VMEM((4, 256, 1024), BF16),
            pltpu.VMEM((32, 2, 256), BF16),
            pltpu.VMEM((128, 128), BF16),
            pltpu.SemaphoreType.DMA((4, 5)),
            pltpu.SemaphoreType.DMA((8,)),
        ],
        compiler_params=pltpu.CompilerParams(vmem_limit_bytes=LEAF_BYTES),
        cost_estimate=pl.CostEstimate(flops=1_342_177_280, bytes_accessed=6_000_000, transcendentals=0),
    )(*map(in_hbm, (weights, inverse, rhs, blocks, outer, m3)))


def first_kernel(t1_ref, t2_ref, t3_ref, o_ref, m1_ref, m1r_ref, t2n_ref, t3n_ref, on_ref, d1_ref, kept_ref, near_ref, far_ref, ring_ref, one, shares):
    row = lax.axis_index("srow")
    own = pl.multiple_of((row & 1) * 128, 128)
    other = pl.multiple_of(128 - (row & 1) * 128, 128)
    for slot in range(4):
        into = d1_ref if slot == 0 else one.at[slot - 1]
        into[pl.ds(own, 128), :] = m1_ref[:, slot, :]
        into[pl.ds(other, 128), :] = m1r_ref[:, slot, :]
    x1 = dot(d1_ref[...], t1_ref[...]).astype(BF16)
    under = dot(one[...].reshape(768, 256), x1)
    t2 = t2_ref[...] - under[:256]
    t2n_ref[...] = t2
    for t in range(2):
        first, second = t2[:, t * 128 : (t + 1) * 128], t2[:, (t + 2) * 128 : (t + 3) * 128]
        shares[2 * t] = join_halves(first, second, False)
        shares[2 * t + 1] = join_halves(first, second, True)
    place = row & 3
    for half in range(2):
        near_ref[:, half * 128 : (half + 1) * 128] = own_and_other(t1_ref, half)[1].astype(BF16)
    near_ref[:, 256:] = shares[place ^ 1].astype(BF16)
    kept_ref[...] = shares[place]
    far_ref[...] = shares[place ^ 2].astype(BF16)
    ring_ref[...] = shares[place ^ 3].astype(BF16)
    t3n_ref[...] = t3_ref[...] - under[256:512]
    on_ref[...] = o_ref[...] - under[512:]


def first_level(t1, t2, t3, o, m1, m1r):
    full = pltpu.VMEM((256, 512), F32)
    share = pltpu.VMEM((256, 128), BF16)
    return pl.pallas_call(
        first_kernel,
        name="first",
        out_shape=[
            full, full, full, pltpu.VMEM((256, 256), BF16),
            pltpu.VMEM((256, 128), F32), pltpu.VMEM((256, 384), BF16), share, share,
        ],
        scratch_shapes=[pltpu.VMEM((3, 256, 256), BF16), pltpu.VMEM((4, 256, 128), F32)],
        input_output_aliases={1: 0, 2: 1, 3: 2},
        compiler_params=pltpu.CompilerParams(vmem_limit_bytes=TRANSFORM_BYTES),
        cost_estimate=pl.CostEstimate(flops=270_000_000, bytes_accessed=3_000_000, transcendentals=0),
    )(*map(in_vmem, (t1, t2, t3, o, m1, m1r)))


def second_kernel(t2_ref, t3_ref, o_ref, m2_ref, blocks_ref, a8_hbm, d2_ref, two, a8, sems):
    for q in range(4):
        for slot in range(3):
            into = d2_ref if slot == 0 else two.at[slot - 1]
            into[q * 64 : (q + 1) * 64, :] = m2_ref[q, slot]
    x2 = dot(d2_ref[...], t2_ref[...].astype(BF16)).astype(BF16)
    copies = []
    for half in range(2):
        wide = slice(half * 256, half * 256 + 256)
        above = dot(two[...].reshape(512, 256), x2[:, wide])
        t3 = t3_ref[:, wide] - above[:256]
        o = o_ref[:, wide] - above[256:]
        for i in range(4):
            k = half * 4 + i
            cut = slice(i // 2 * 128, i // 2 * 128 + 128)
            a8[k] = join_halves(t3[:, cut], o[:, cut], i % 2 == 1).astype(BF16)
            copies.append(pltpu.make_async_copy(a8.at[k], a8_hbm.at[k, :256], sems.at[k]))
            copies[-1].start()
    for copy in copies:
        copy.wait()


def second_level(t2, t3, o, m2, blocks):
    return pl.pallas_call(
        second_kernel,
        name="second",
        in_specs=[pl.BlockSpec(memory_space=pltpu.VMEM)] * 4 + [pl.BlockSpec(memory_space=pl.ANY)],
        out_specs=[pl.BlockSpec(memory_space=pl.ANY), pl.BlockSpec(memory_space=pltpu.VMEM)],
        out_shape=[pltpu.HBM((8, 384, 128), BF16), pltpu.VMEM((256, 256), BF16)],
        scratch_shapes=[
            pltpu.VMEM((2, 256, 256), BF16),
            pltpu.VMEM((8, 256, 128), BF16),
            pltpu.SemaphoreType.DMA((8,)),
        ],
        input_output_aliases={4: 0},
        compiler_params=pltpu.CompilerParams(vmem_limit_bytes=TRANSFORM_BYTES),
        cost_estimate=pl.CostEstimate(flops=200_000_000, bytes_accessed=3_000_000, transcendentals=0),
    )(*map(in_vmem, (t2, t3, o, m2)), in_hbm(blocks))


def third_kernel(r8_ref, x3_ref, out_ref, d3, l3, v):
    total = r8_ref[0, :256].astype(F32)
    for k in range(1, 8):
        total = total + r8_ref[k, :256].astype(F32)
    for k in range(8):
        for side in range(2):
            cut = slice(side * 128, (side + 1) * 128)
            start = 256 + side * 64
            d3[k * 32 : (k + 1) * 32, cut] = r8_ref[k, start : start + 32]
            l3[k * 32 : (k + 1) * 32, cut] = r8_ref[k, start + 32 : start + 64]
    x3 = -dot_wide(d3[...], total)
    x3_ref[...] = jnp.transpose(x3)[:64, :].astype(BF16)
    v[...] = total + pltpu.roll(dot_wide(l3[...], x3), 64, 1)
    low = low_lanes((8, 128))
    for p in range(16):
        upper, lower = v[p * 16 : p * 16 + 8, :], v[p * 16 + 8 : p * 16 + 16, :]
        out_ref[p] = jnp.where(low, pltpu.roll(upper, 64, 1), lower).astype(BF16)


def third_level(r8):
    return pl.pallas_call(
        third_kernel,
        name="third",
        out_shape=[
            jax.ShapeDtypeStruct((64, 256), BF16),
            pltpu.VMEM((16, 8, 128), BF16),
        ],
        scratch_shapes=[pltpu.VMEM((256, 256), BF16), pltpu.VMEM((256, 256), BF16), pltpu.VMEM((256, 128), F32)],
        compiler_params=pltpu.CompilerParams(vmem_limit_bytes=SMALL_BYTES),
        cost_estimate=pl.CostEstimate(flops=70_000_000, bytes_accessed=1, transcendentals=0),
    )(in_vmem(r8))


def lower_kernel(t1_ref, kept_ref, near_ref, far_ref, ring_ref, d1_ref, d2_ref, x1_ref, x2_ref):
    kept_one = jnp.concatenate([own_and_other(t1_ref, half)[0] for half in range(2)], axis=1)
    x1_ref[...] = (-dot_wide(d1_ref[...], kept_one + near_ref[:, :256].astype(F32))).astype(BF16)
    sum_two = kept_ref[...] + near_ref[:, 256:].astype(F32)
    sum_two = sum_two + far_ref[...].astype(F32) + ring_ref[...].astype(F32)
    x2_ref[...] = (-dot_wide(d2_ref[...], sum_two)).astype(BF16)


def lower_levels(t1, kept, near, far, ring, d1, d2):
    return pl.pallas_call(
        lower_kernel,
        name="lower",
        out_shape=[jax.ShapeDtypeStruct((256, 256), BF16), jax.ShapeDtypeStruct((256, 128), BF16)],
        compiler_params=pltpu.CompilerParams(vmem_limit_bytes=SMALL_BYTES),
        cost_estimate=pl.CostEstimate(flops=1, bytes_accessed=1, transcendentals=0),
    )(*map(in_vmem, (t1, kept, near, far, ring, d1, d2)))


def final_kernel(r_ref, after_ref, out_ref):
    total = r_ref[0].astype(F32)
    for k in range(1, 16):
        total = total + r_ref[k].astype(F32)
    out_ref[0:8, :] = total[:, :64]
    out_ref[8:16, :] = pltpu.roll(total, 64, 1)[:, :64]


def final_sum(received, after):
    return pl.pallas_call(
        final_kernel,
        name="final",
        in_specs=[pl.BlockSpec(memory_space=pltpu.VMEM), pl.BlockSpec(memory_space=pl.ANY)],
        out_shape=jax.ShapeDtypeStruct((16, 64), F32),
        compiler_params=pltpu.CompilerParams(vmem_limit_bytes=SMALL_BYTES),
        cost_estimate=pl.CostEstimate(flops=20_000, bytes_accessed=40_000, transcendentals=0),
    )(in_vmem(received), in_hbm(after))


def swap(block, flip):
    return lax.ppermute(block, "srow", [(i, i ^ flip) for i in range(32)])


def shards(
    leaf_rhs, leaf_inverse, leaf_blocks, leaf_outer, leaf_targets, level_one, level_two, level_three
):
    m1, m3 = level_one[:, 0], level_three[:, 0]
    m1r = swap(m1, 1)
    m2 = spread(jnp.transpose(level_two[:, 0], (1, 0, 2)))
    m2 = lax.all_to_all(m2, "srow", 0, 0, axis_index_groups=GROUPS_4, tiled=True)
    t1, t2, t3, o, a8 = leaf_terms(
        leaf_targets[0, 0], leaf_inverse[0, 0], leaf_rhs[0, 0], leaf_blocks[0, 0], leaf_outer[0, 0], m3
    )
    t2, t3, o, d1, kept, near, far, ring = first_level(t1, t2, t3, o, m1, m1r)
    a8, d2 = second_level(t2, t3, o, m2, a8)
    r8 = lax.all_to_all(a8, "srow", 0, 0, axis_index_groups=GROUPS_8, tiled=True)
    x3, parts = third_level(r8)
    received = lax.all_to_all(parts, "scol", 0, 0, tiled=True)
    x1, x2 = lower_levels(t1, kept, swap(near, 1), swap(far, 2), swap(ring, 3), d1, d2)
    outer_update = final_sum(received, x2)
    return (x1[:, None, :], x2[:, None, :], jnp.transpose(x3)[:, None, :], outer_update)


def solution(mesh):
    placed = (
        P("srow", "scol", None, None, None),
        P("srow", "scol", None, None, None),
        P("srow", "scol", None, None, None, None),
        P("srow", "scol", None, None, None),
        P("srow", "scol", None, None),
        P("srow", "scol", None, None),
        P("srow", "scol", None, None),
        P("srow", "scol", None, None),
    )
    return jax.shard_map(
        shards,
        mesh=mesh,
        in_specs=placed,
        out_specs=(
            P(None, "scol", "srow"),
            P(None, "scol", "srow"),
            P(None, "scol", "srow"),
            P("scol", "srow"),
        ),
        check_vma=False,
    )
```
